32 devices in a mesh: dp: 8 (over y, x, core), slab: 4 (over z).
Axes of the slice: x: 2, y: 2, z: 4, core: 2. Of those that a mesh axis runs over, the one named last changes fastest.
Arguments:
- activation: bfloat16 [32, 64, 128, 256], P('dp', None, 'slab'), may hold values from -6 to 6
- cotangent: bfloat16 [32, 64, 128, 256], P('dp', None, 'slab'), may hold values from -6 to 6
- spectral_weight: bfloat16 [64, 32, 32, 128], P(None, 'slab'), may hold values from -0.75 to 0.75
Outputs:
- input_grad: bfloat16 [32, 64, 128, 256], P('dp', None, 'slab')
- weight_grad: float32 [64, 32, 32, 128], P('dp', 'slab')
The draws below stay inside these ranges and needn't reach their ends.
All inputs are finite; a program needn't handle non-finite values.
Results may differ from the reference program's by a relative error of at most 0.023.
Values may be sent and summed in bfloat16 or wider, within the bound.
No kernel may reach another device: no remote copies, remote signals or barrier semaphores. Data moves between devices by JAX's collectives and lax.ppermute only.
A program may use at most 64 MiB of HBM per device.

```python
import math
import jax
import jax.numpy as jnp

C = 64
X = 128
Y = 128
MX = 32
MY = 32
BATCH = 32


def strengthened(values, own_key, source, target, shards_of, factor):
    owner, partner = [(jnp.arange(values.shape[position]) // (values.shape[position] // shards_of)).reshape([-1 if axis == position else 1 for axis in range(values.ndim)]) for position in (source, target)]
    chosen = jax.random.permutation(own_key, shards_of)[partner]
    strong = (owner == chosen) | (owner == (partner + shards_of // 2) % shards_of)
    return jnp.where(strong, factor * values, values)


def steps_of(own_key, extent, shards, smallest, largest):
    def one(dim, shards_of):
        steps = jax.random.uniform(jax.random.fold_in(jax.random.fold_in(own_key, 6), dim), (shards_of,), jnp.float32, smallest / len(shards), largest / len(shards))
        return jnp.repeat(jnp.exp(steps), extent[dim] // shards_of).reshape((-1,) + (1,) * (len(extent) - dim - 1))

    loudness = one(*shards[0])
    for cut in shards[1:]:
        loudness = loudness * one(*cut)
    return loudness


def centred(rng, extent, scale, bound, cuts=(), held_as=jnp.bfloat16):
    loudness = steps_of(rng, extent, cuts, -0.22, 0.18) if cuts else 1.0
    entries = jax.random.normal(rng, extent, jnp.float32) * scale * loudness
    return jnp.minimum(jnp.maximum(entries, -bound), bound).astype(held_as)


def bell_draw_with(own_key, shape, scale, bound, pieces, heavy, kind=jnp.bfloat16):
    array = scale * jax.random.normal(own_key, shape, jnp.float32)
    if pieces:
        array = array * steps_of(own_key, shape, pieces, -0.22, 0.18)
    return jnp.clip(strengthened(array, jax.random.fold_in(own_key, 3), *heavy), -bound, bound).astype(kind)


def setup_inputs(seed: int = 0) -> dict:
    splits = jax.random.split(jax.random.key(seed), 4)
    return {
        "activation": bell_draw_with(splits[0], (BATCH, C, X, 2 * Y), 1.0, 6.0, ((0, 8), (2, 4)), (0, 1, 8, 2.0)),
        "cotangent": centred(splits[1], (BATCH, C, X, 2 * Y), 1.0, 6.0, ((0, 8), (2, 4))),
        "spectral_weight": centred(splits[2], (C, MY, MX, 2 * C), C ** -0.5, 0.75, ((1, 4),)),
    }


def retained(length, modes):
    index = jnp.arange(modes, dtype=jnp.int32)
    return jnp.where(index < modes // 2, index, index + (length - modes))

def cos_sin(length, modes):
    cells = jnp.arange(length, dtype=jnp.int32)
    phase = cells[:, None] * retained(length, modes)[None, :] % length
    angle = phase.astype(jnp.float32) * (2.0 * math.pi / length)
    factor = 1.0 / math.sqrt(length)
    return ((jnp.cos(angle) * factor).astype(jnp.bfloat16), (jnp.sin(angle) * factor).astype(jnp.bfloat16))

def y_table(cosine_table, sine_table):
    upper = jnp.concatenate([cosine_table, -sine_table], axis=1)
    lower = jnp.concatenate([sine_table, cosine_table], axis=1)
    return jnp.concatenate([upper, lower], axis=0)

def x_table(cosine_table, sine_table):
    first = jnp.stack([cosine_table, -sine_table], axis=2)
    second = jnp.stack([sine_table, cosine_table], axis=2)
    return jnp.stack([first, second], axis=1)

def reference(activation, cotangent, spectral_weight):
    cos_y, sin_y = cos_sin(Y, MY)
    cos_x, sin_x = cos_sin(X, MX)
    table_y = y_table(cos_y, sin_y)
    table_x = x_table(cos_x, sin_x).astype(jnp.float32)

    def spectrum(volume):
        lines = volume.reshape(-1, 2 * Y)
        along = jnp.dot(lines, table_y, preferred_element_type=jnp.float32).astype(jnp.bfloat16)
        along = along.reshape(BATCH, C, X, 2, MY).astype(jnp.float32)
        return jnp.einsum('bcxpt,xpkq->bckqt', along, table_x).astype(jnp.bfloat16)
    spec_in = spectrum(activation).astype(jnp.float32)
    spec_out = spectrum(cotangent).astype(jnp.float32)
    swapped = jnp.stack([spec_out[:, :, :, 1], -spec_out[:, :, :, 0]], axis=3)
    real_part = jnp.einsum('bikpt,bokpt->itko', spec_in, spec_out)
    imag_part = jnp.einsum('bikpt,bokpt->itko', spec_in, swapped)
    weight_grad = jnp.stack([real_part, imag_part], axis=3).reshape(C, MY, MX, 2 * C)
    weight = spectral_weight.astype(jnp.float32).reshape(C, MY, MX, 2, C)
    grad_real = jnp.einsum('bokpt,itkpo->bikt', spec_out, weight)
    grad_imag = jnp.einsum('bokpt,itkpo->bikt', swapped, weight)
    spec_grad = jnp.stack([grad_real, grad_imag], axis=3).astype(jnp.bfloat16).astype(jnp.float32)
    spread = jnp.einsum('bikqt,xpkq->bixpt', spec_grad, table_x).astype(jnp.bfloat16)
    lines = spread.reshape(-1, 2 * MY)
    values = jnp.dot(lines, table_y.T, preferred_element_type=jnp.float32).astype(jnp.bfloat16)
    input_grad = values.reshape(BATCH, C, X, 2 * Y)
    return (input_grad, weight_grad)
```

```python
import math

import jax
import jax.numpy as jnp
import numpy as np
from jax import lax
from jax.experimental import pallas as pl
from jax.experimental.pallas import tpu as pltpu
from jax.sharding import PartitionSpec as P


def retained(length, modes):
    index = jnp.arange(modes, dtype=jnp.int32)
    return jnp.where(index < modes // 2, index, index + (length - modes))


def cos_sin(length, modes):
    cells = jnp.arange(length, dtype=jnp.int32)
    phase = cells[:, None] * retained(length, modes)[None, :] % length
    angle = phase.astype(jnp.float32) * (2.0 * math.pi / length)
    factor = 1.0 / math.sqrt(length)
    return (
        (jnp.cos(angle) * factor).astype(jnp.bfloat16),
        (jnp.sin(angle) * factor).astype(jnp.bfloat16),
    )


def y_table(cosine_table, sine_table):
    upper = jnp.concatenate([cosine_table, -sine_table], axis=1)
    lower = jnp.concatenate([sine_table, cosine_table], axis=1)
    return jnp.concatenate([upper, lower], axis=0)


def x_table(cosine_table, sine_table):
    first = jnp.stack([cosine_table, -sine_table], axis=2)
    second = jnp.stack([sine_table, cosine_table], axis=2)
    return jnp.stack([first, second], axis=1)


def paired_out(spectra_out, channels):
    modes_here, amount, modes_x = spectra_out.shape[:3]
    split = spectra_out.reshape(modes_here, amount, modes_x, 2, channels)
    swapped = jnp.stack([split[:, :, :, 1], -split[:, :, :, 0]], axis=3)
    return jnp.concatenate([split, swapped], axis=4)


def plain_body(activation, cotangent, spectral_weight):
    slabs = lax.axis_size("slab")
    samples, channels, rows_here, double_y = activation.shape
    y_length = double_y // 2
    x_length = rows_here * slabs
    modes_here = spectral_weight.shape[1]
    modes_y = modes_here * slabs
    modes_x = spectral_weight.shape[2]
    cos_y, sin_y = cos_sin(y_length, modes_y)
    cos_x, sin_x = cos_sin(x_length, modes_x)
    table_y = y_table(cos_y, sin_y).reshape(2 * y_length, 2, slabs, modes_here)
    table_y = table_y.transpose(0, 2, 1, 3).reshape(2 * y_length, 2 * modes_y)
    table_x = x_table(cos_x, sin_x)
    table_slabs = table_x.reshape(slabs, rows_here, 2, modes_x, 2)

    def to_modes(volume):
        along = jnp.einsum("ys,bcry->sbcr", table_y, volume, preferred_element_type=jnp.float32)
        along = along.astype(jnp.bfloat16)
        return along.reshape(slabs, 2 * modes_here, samples, channels * rows_here)

    members = (
        lax.all_to_all(to_modes(activation), "slab", split_axis=0, concat_axis=0, tiled=True),
        lax.all_to_all(to_modes(cotangent), "slab", split_axis=0, concat_axis=0, tiled=True),
    )
    results = []
    for member in members:
        amount = member.shape[2]
        layout = member.reshape(slabs, 2, modes_here, amount, channels, rows_here)
        spectra = jnp.einsum(
            "sptbcr,srpkq->tbkqc", layout, table_slabs, preferred_element_type=jnp.float32
        )
        results.append(
            spectra.astype(jnp.bfloat16).reshape(modes_here, amount, modes_x, 2 * channels)
        )
    spec_in, spec_out = tuple(results)
    inputs_split = spec_in.reshape(modes_here, samples, modes_x, 2, channels)
    paired = paired_out(spec_out, channels)
    weight_grad = lax.psum_scatter(
        jnp.einsum(
            "tbkqi,tbkqn->itkn", inputs_split, paired, preferred_element_type=jnp.float32
        ).astype(jnp.bfloat16),
        "dp",
        scatter_dimension=0,
        tiled=True,
    ).astype(jnp.float32)
    inputs_paired = paired_out(spec_out, channels)
    stacked = jnp.stack([inputs_paired[..., :channels], inputs_paired[..., channels:]], axis=3)
    stacked = stacked.transpose(0, 1, 2, 4, 3, 5).reshape(
        modes_here, samples, modes_x, 2, 2 * channels
    )
    spec_grad = jnp.einsum(
        "tbkrn,itkn->tbkri", stacked, spectral_weight, preferred_element_type=jnp.float32
    )
    spec_grad = spec_grad.astype(jnp.bfloat16)
    spread = jnp.einsum(
        "tbkqi,srpkq->sptbir", spec_grad, table_slabs, preferred_element_type=jnp.float32
    )
    spread = spread.astype(jnp.bfloat16).reshape(
        slabs, 2 * modes_here, samples, channels * rows_here
    )
    member = lax.all_to_all(spread, "slab", split_axis=0, concat_axis=0, tiled=True)
    amount = member.shape[2]
    lines = member.reshape(2 * modes_y, amount, channels, rows_here)
    values = jnp.einsum("sbcr,ys->bcry", lines, table_y, preferred_element_type=jnp.float32)
    input_grad = values.astype(jnp.bfloat16)
    return (input_grad, weight_grad)


NT = (((1,), (1,)), ((), ()))
TN = (((0,), (0,)), ((), ()))
PAIR = 2
PARTS = 2
BLOCK = 16
VMEM_BYTES = 12 * 2**20
F32 = jnp.float32
BF16 = jnp.bfloat16


def tables(length, modes):
    index = np.arange(modes)
    kept = np.where(index < modes // 2, index, index + (length - modes))
    phase = (np.arange(length)[:, None] * kept[None, :]) % length
    angle = (phase.astype(np.float32) * np.float32(2.0 * math.pi / length)).astype(np.float64)
    factor = 1.0 / math.sqrt(length)
    return np.cos(angle) * factor, np.sin(angle) * factor


def y_constant(y_length, modes_y, slabs, parts):
    cosine, sine = tables(y_length, modes_y)
    real = np.concatenate([cosine, sine], axis=0).T
    imag = np.concatenate([-sine, cosine], axis=0).T
    both = []
    for one, other in ((real, imag), (imag, -real)):
        pair = np.stack([one, other]).reshape(2, slabs, parts, -1, 2 * y_length)
        both.append(pair.transpose(1, 2, 0, 3, 4).reshape(slabs, -1, 2 * y_length))
    order = [[d ^ m for m in range(slabs)] for d in range(slabs)]
    rows = [np.concatenate([table[o].reshape(-1, 2 * y_length) for table in both]) for o in order]
    return jnp.asarray(np.stack(rows), BF16)


def x_constants(x_length, modes_x, slabs, copies):
    cosine, sine = tables(x_length, modes_x)
    rows_here = x_length // slabs
    eye = np.eye(copies)
    forward = []
    for d in range(slabs):
        own = slice(d * rows_here, (d + 1) * rows_here)
        forward.append(np.concatenate([np.kron(eye, cosine[own]), np.kron(eye, sine[own])]))
    forward = np.stack(forward)
    half = copies * rows_here
    split = (slabs, 2 * half, PAIR, copies // PAIR, modes_x // BLOCK, BLOCK)
    forward = forward.reshape(split).transpose(0, 1, 2, 4, 3, 5).reshape(slabs, 2 * half, -1)
    backward = np.concatenate(
        [forward[:, :half].transpose(0, 2, 1), forward[:, half:].transpose(0, 2, 1)], axis=2
    )
    return jnp.asarray(forward, BF16), jnp.asarray(backward, BF16)


def to_spectrum(volume, table_y, table_x, slab, pieces):
    samples, channels, rows, double_y = volume.shape
    height = table_y.shape[1] // 2
    group = height // pieces
    wide = table_x.shape[2]
    tall = table_x.shape[1] // 2
    step = min(channels, 32)
    tiles = step // PAIR

    def kernel(slab_ref, v_ref, y_ref, x_ref, *refs):
        outs, mixed = refs[:pieces], refs[pieces]
        for tile in range(tiles):
            block = jnp.concatenate(
                [v_ref[b, tile * PAIR + c] for c in range(PAIR) for b in range(samples)], axis=0
            )
            along = lax.dot_general(y_ref[0], block, NT, preferred_element_type=F32).astype(BF16)
            here = slice(tile * height, (tile + 1) * height)
            mixed[here, :tall] = along[:height]
            mixed[here, tall:] = along[height:]
        spectra = jnp.dot(mixed[...], x_ref[0], preferred_element_type=F32).astype(BF16)
        for tile in range(tiles):
            for m in range(pieces):
                first = tile * height + m * group
                outs[m][:, tile * wide : (tile + 1) * wide] = spectra[first : first + group]

    lanes = channels // PAIR * wide
    return pl.pallas_call(
        kernel,
        out_shape=[jax.ShapeDtypeStruct((group, lanes), BF16)] * pieces,
        grid_spec=pltpu.PrefetchScalarGridSpec(
            num_scalar_prefetch=1,
            grid=(channels // step,),
            in_specs=[
                pl.BlockSpec((samples, step, rows, double_y), lambda n, s: (0, n, 0, 0)),
                pl.BlockSpec((1,) + table_y.shape[1:], lambda n, s: (s[0], 0, 0)),
                pl.BlockSpec((1,) + table_x.shape[1:], lambda n, s: (s[0], 0, 0)),
            ],
            out_specs=[pl.BlockSpec((group, tiles * wide), lambda n, s: (0, n))] * pieces,
            scratch_shapes=[pltpu.VMEM((tiles * height, 2 * tall), BF16)],
        ),
        compiler_params=pltpu.CompilerParams(vmem_limit_bytes=VMEM_BYTES),
        name="to_spectrum",
        cost_estimate=pl.CostEstimate(
            flops=2 * volume.size * height, bytes_accessed=2 * volume.size, transcendentals=0
        ),
    )(slab, volume, table_y, table_x)


def turn(block, half):
    return jnp.concatenate([block[half:], -block[:half]], axis=0)


def lane_masks(width):
    lane = lax.broadcasted_iota(jnp.int32, (BLOCK, width), 1)
    same = lane % BLOCK == lax.broadcasted_iota(jnp.int32, (BLOCK, width), 0)
    return same & (lane < width // 2), same & (lane >= width // 2)


def apply_weight(parts, weight):
    channels_in, modes, _, double_c = weight.shape
    channels = double_c // 2
    group, lanes = parts[0].shape
    width = lanes // channels
    step = min(channels_in, 16)
    chunks = channels_in // step
    pairs = modes // PARTS
    count = len(parts)

    def kernel(*refs):
        part_refs = refs[:count]
        w_ref, grad_ref, spec_ref, spread, right, picked = refs[count:]
        for c in range(channels):
            here = slice(c * width, (c + 1) * width)
            total = part_refs[0][:, here].astype(F32)
            for ref in part_refs[1:]:
                total = total + ref[:, here].astype(F32)
            for h in range(PARTS):
                spread[pl.ds(h * channels + c, 2 * pairs, stride=double_c), :] = total[
                    h * 2 * pairs : (h + 1) * 2 * pairs
                ]
        lower = lax.broadcasted_iota(jnp.int32, (double_c, width), 1) < width // 2
        right[...] = jnp.zeros_like(right)
        for p in range(pairs):
            for h in range(PARTS):
                first = p * double_c + h * channels
                second = first + pairs * double_c
                block = jnp.concatenate(
                    [spread[first : first + channels, :], spread[second : second + channels, :]],
                    axis=0,
                )
                spec_ref[h * pairs + p] = block.astype(BF16)
                turned = pltpu.roll(turn(block, channels), width // 2, 1)
                rows = slice(h * double_c, (h + 1) * double_c)
                columns = slice(h * width, (h + 1) * width)
                right[p, 0, rows, columns] = jnp.where(lower, block, turned).astype(BF16)
                right[p, 1, rows, columns] = jnp.where(lower, turned, block).astype(BF16)

        masks = [[m[8 * v : 8 * v + 8] for v in range(BLOCK // 8)] for m in lane_masks(width)]
        rows = lax.broadcasted_iota(jnp.int32, (group, group * 8), 0)
        columns = lax.broadcasted_iota(jnp.int32, (group, group * 8), 1)
        ones = jnp.where(columns // 8 == rows, 1.0, 0.0).astype(BF16)
        real = lax.broadcasted_iota(jnp.int32, (group, width), 0) % (2 * pairs) < pairs

        @pl.loop(0, chunks)
        def _(n):
            rows_here = pl.ds(n * step, step)
            for p in range(pairs):
                full = []
                for k in range(2):
                    left = jnp.concatenate(
                        [
                            w_ref[rows_here, h * pairs + p, k * BLOCK : (k + 1) * BLOCK].reshape(
                                step * BLOCK, double_c
                            )
                            for h in range(PARTS)
                        ],
                        axis=1,
                    )
                    full.append(jnp.dot(left, right[p, k], preferred_element_type=F32))
                for i in range(step):
                    for h in range(PARTS):
                        for r in range(2):
                            kept = jnp.zeros((8, width), F32)
                            for k in range(2):
                                for v in range(BLOCK // 8):
                                    first = i * BLOCK + 8 * v
                                    kept = jnp.where(
                                        masks[k ^ r][v],
                                        full[k][first : first + 8, h * width : (h + 1) * width],
                                        kept,
                                    )
                            at = ((h * 2 + r) * pairs + p) * 8
                            picked[at : at + 8, i * width : (i + 1) * width] = kept
            grad = jnp.dot(ones, picked[...].astype(BF16), preferred_element_type=F32)
            for i in range(step):
                piece = grad[:, i * width : (i + 1) * width]
                piece = jnp.where(real, piece, pltpu.roll(piece, width // 2, 1))
                at = pl.multiple_of(n * (step * width), step * width) + i * width
                grad_ref[:, pl.ds(at, width)] = piece.astype(BF16)

    return pl.pallas_call(
        kernel,
        out_shape=[
            jax.ShapeDtypeStruct((group, channels_in * width), BF16),
            jax.ShapeDtypeStruct((modes, double_c, width), BF16),
        ],
        in_specs=[pl.BlockSpec(memory_space=pltpu.VMEM)] * (count + 1),
        out_specs=[pl.BlockSpec(memory_space=pltpu.VMEM)] * 2,
        scratch_shapes=[
            pltpu.VMEM((modes * double_c, width), F32),
            pltpu.VMEM((pairs, 2, PARTS * double_c, PARTS * width), BF16),
            pltpu.VMEM((group * 8, step * width), F32),
        ],
        compiler_params=pltpu.CompilerParams(vmem_limit_bytes=VMEM_BYTES),
        name="apply_weight",
        cost_estimate=pl.CostEstimate(
            flops=4 * weight.size * width, bytes_accessed=2 * weight.size, transcendentals=0
        ),
    )(*parts, weight)


def split_channels(parts, place, shares):
    group, lanes = parts[0].shape
    width = lanes // shares
    count = len(parts)

    def kernel(place_ref, *refs):
        outs = refs[count:]
        for m in range(shares):
            first = pl.multiple_of((place_ref[0] ^ m) * width, width)
            total = refs[0][:, pl.ds(first, width)].astype(F32)
            for ref in refs[1:count]:
                total = total + ref[:, pl.ds(first, width)].astype(F32)
            outs[m][...] = total.astype(BF16)

    return pl.pallas_call(
        kernel,
        out_shape=[jax.ShapeDtypeStruct((group, width), BF16)] * shares,
        in_specs=[pl.BlockSpec(memory_space=pltpu.SMEM)]
        + [pl.BlockSpec(memory_space=pltpu.VMEM)] * count,
        out_specs=[pl.BlockSpec(memory_space=pltpu.VMEM)] * shares,
        compiler_params=pltpu.CompilerParams(vmem_limit_bytes=VMEM_BYTES),
        name="split_channels",
    )(place, *parts)


def from_spectrum(slots, table_y, table_x, slab, shape):
    samples, channels, rows, double_y = shape
    height = table_y.shape[1] // 2
    group = height // len(slots)
    share = group // PARTS
    deep = table_x.shape[1]
    tall = table_x.shape[2] // 2
    step = min(channels, 32)
    tiles = step // PAIR
    flat = [piece for slot in slots for piece in slot]
    sizes = [len(slot) for slot in slots]

    def kernel(slab_ref, *refs):
        pieces = refs[: len(flat)]
        y_ref, x_ref, out_ref, held = refs[len(flat) :]
        sign = jnp.where(
            lax.broadcasted_iota(jnp.int32, (height, tall), 0) % share < share // 2, -1.0, 1.0
        )
        for tile in range(tiles):
            here = slice(tile * deep, (tile + 1) * deep)
            at = 0
            for m, size in enumerate(sizes):
                block = pieces[at][:, here]
                for extra in pieces[at + 1 : at + size]:
                    block = block + extra[:, here]
                at += size
                held[tile * height + m * group : tile * height + (m + 1) * group, :] = block
        both = jnp.dot(held[...], x_ref[0], preferred_element_type=F32)
        for tile in range(tiles):
            here = slice(tile * height, (tile + 1) * height)
            other = both[here, tall:].reshape(height // share, share, tall)
            other = pltpu.roll(other, share // 2, 1).reshape(height, tall)
            spread = (both[here, :tall] + sign * other).astype(BF16)
            values = lax.dot_general(
                spread, y_ref[0, :height], TN, preferred_element_type=F32
            ).astype(BF16)
            for c in range(PAIR):
                for b in range(samples):
                    at = (c * samples + b) * rows
                    out_ref[b, tile * PAIR + c] = values[at : at + rows]

    return pl.pallas_call(
        kernel,
        out_shape=jax.ShapeDtypeStruct(shape, BF16),
        grid_spec=pltpu.PrefetchScalarGridSpec(
            num_scalar_prefetch=1,
            grid=(channels // step,),
            in_specs=[pl.BlockSpec((group, tiles * deep), lambda n, s: (0, n))] * len(flat)
            + [
                pl.BlockSpec((1,) + table_y.shape[1:], lambda n, s: (s[0], 0, 0)),
                pl.BlockSpec((1,) + table_x.shape[1:], lambda n, s: (s[0], 0, 0)),
            ],
            out_specs=pl.BlockSpec((samples, step, rows, double_y), lambda n, s: (0, n, 0, 0)),
            scratch_shapes=[pltpu.VMEM((tiles * height, deep), BF16)],
        ),
        compiler_params=pltpu.CompilerParams(vmem_limit_bytes=VMEM_BYTES),
        name="from_spectrum",
        cost_estimate=pl.CostEstimate(
            flops=2 * math.prod(shape) * height,
            bytes_accessed=2 * math.prod(shape),
            transcendentals=0,
        ),
    )(slab, *flat, table_y, table_x)


def correlate(inputs, outputs, modes_x):
    shares = len(inputs)
    group, lanes = inputs[0].shape
    modes, double_c, width = outputs[0].shape
    own = lanes // width

    pairs = modes // PARTS

    def kernel(*refs):
        in_refs, out_refs = refs[:shares], refs[shares : 2 * shares]
        grad_ref, rows, turned_rows, left, right = refs[2 * shares :]
        for m in range(shares):
            here = slice(m * group, (m + 1) * group)
            rows[here, :] = in_refs[m][...].astype(F32)
            for i in range(own):
                lanes_here = slice(i * width, (i + 1) * width)
                turned_rows[here, lanes_here] = pltpu.roll(rows[here, lanes_here], width // 2, 1)
        masks = lane_masks(width)
        lower = lax.broadcasted_iota(jnp.int32, (double_c, width), 1) < width // 2

        @pl.loop(0, modes, unroll=modes)
        def _(j):
            slot = j % 2
            for m in range(shares):
                block = out_refs[m][j]
                turned = pltpu.roll(turn(block, double_c // 2).astype(F32), width // 2, 1).astype(BF16)
                here = slice(m * width, (m + 1) * width)
                right[slot, 0, :, here] = jnp.where(lower, block, turned)
                right[slot, 1, :, here] = jnp.where(lower, turned, block)
                at = m * group + j // pairs * (2 * pairs) + j % pairs
                one = rows[pl.ds(at, 1), :]
                other = turned_rows[pl.ds(at + pairs, 1), :]
                for i in range(own):
                    lanes_here = slice(i * width, (i + 1) * width)
                    real = jnp.broadcast_to(one[:, lanes_here], (BLOCK, width))
                    imag = jnp.broadcast_to(other[:, lanes_here], (BLOCK, width))
                    for k in range(2):
                        left[slot, k, i * BLOCK : (i + 1) * BLOCK, here] = jnp.where(
                            masks[k], real, jnp.where(masks[1 - k], imag, 0.0)
                        ).astype(BF16)
            for k in range(2):
                result = lax.dot_general(
                    left[slot, k], right[slot, k], NT, preferred_element_type=F32
                )
                for i in range(own):
                    grad_ref[i, j, k * BLOCK : (k + 1) * BLOCK] = result[
                        i * BLOCK : (i + 1) * BLOCK
                    ]

    return pl.pallas_call(
        kernel,
        out_shape=jax.ShapeDtypeStruct((own, modes, modes_x, double_c), F32),
        in_specs=[pl.BlockSpec(memory_space=pltpu.VMEM)] * (2 * shares),
        out_specs=pl.BlockSpec(memory_space=pltpu.VMEM),
        scratch_shapes=[
            pltpu.VMEM((shares * group, lanes), F32),
            pltpu.VMEM((shares * group, lanes), F32),
            pltpu.VMEM((2, 2, own * BLOCK, shares * width), BF16),
            pltpu.VMEM((2, 2, double_c, shares * width), BF16),
        ],
        compiler_params=pltpu.CompilerParams(vmem_limit_bytes=VMEM_BYTES),
        name="correlate",
        cost_estimate=pl.CostEstimate(
            flops=2 * own * modes * modes_x * double_c * shares * width,
            bytes_accessed=2 * shares * modes * double_c * width,
            transcendentals=0,
        ),
    )(*inputs, *outputs)


def swap(value, axis, bits):
    size = lax.axis_size(axis)
    return lax.ppermute(value, axis, [(d, d ^ bits) for d in range(size)])


def centre(value):
    return lax.ppermute(value, "slab", [(1, 2), (2, 1)])


def add(one, other):
    def kernel(one_ref, other_ref, sum_ref):
        sum_ref[...] = (one_ref[...].astype(F32) + other_ref[...].astype(F32)).astype(BF16)

    return pl.pallas_call(
        kernel,
        out_shape=jax.ShapeDtypeStruct(one.shape, BF16),
        in_specs=[pl.BlockSpec(memory_space=pltpu.VMEM)] * 2,
        out_specs=pl.BlockSpec(memory_space=pltpu.VMEM),
        compiler_params=pltpu.CompilerParams(vmem_limit_bytes=VMEM_BYTES),
        name="add",
        cost_estimate=pl.CostEstimate(flops=one.size, bytes_accessed=6 * one.size, transcendentals=0),
    )(one, other)


def fast_body(activation, cotangent, spectral_weight):
    slabs = lax.axis_size("slab")
    groups = lax.axis_size("dp")
    samples, _, rows_here, double_y = activation.shape
    modes_here, modes_x = spectral_weight.shape[1:3]
    table_y = y_constant(double_y // 2, modes_here * slabs, slabs, PARTS)
    forward_x, backward_x = x_constants(rows_here * slabs, modes_x, slabs, PAIR * samples)
    slab = lax.axis_index("slab").astype(jnp.int32).reshape(1)
    place = lax.axis_index("dp").astype(jnp.int32).reshape(1)
    distances = sorted(range(1, slabs), reverse=True)

    def exchange(values):
        return [swap(values[m], "slab", m) for m in distances]

    def gather_terms(own):
        far = swap(own[3], "slab", 1)
        skip = swap(own[2], "slab", 1)
        middle = centre(add(own[2], far))
        last = centre(add(own[3], skip))
        near = swap(add(own[1], middle), "slab", 1)
        return [own[0], near, last]

    first = [pltpu.with_memory_space_constraint(v, pltpu.HBM) for v in (cotangent, table_y, forward_x)]
    parts_out = to_spectrum(*first, slab, slabs)
    terms_out = [parts_out[0]] + exchange(parts_out)
    parts_in = to_spectrum(activation, table_y, forward_x, slab, slabs)
    grad, spec_out = apply_weight(terms_out, spectral_weight)
    terms_in = gather_terms(parts_in)
    received = exchange([grad] * slabs)
    grads = [grad] + received[::-1]

    everyone = [spec_out] + [None] * (groups - 1)
    for m in [*range(groups - 2, 0, -2), *range(1, groups, 2)]:
        source, bits = (everyone[m - 1], 1) if m % 2 else (spec_out, m)
        everyone[m] = swap(source, "dp", bits)
    pieces = split_channels(terms_in, place, groups)
    pieces = [pieces[0]] + [swap(pieces[m], "dp", m) for m in range(1, groups)]
    weight_grad = correlate(pieces, everyone, modes_x)
    input_grad = from_spectrum(
        [[piece] for piece in grads], table_y, backward_x, slab, activation.shape
    )
    return (input_grad, weight_grad)


def fits(mesh, activation, spectral_weight):
    slabs, groups = mesh.shape["slab"], mesh.shape["dp"]
    samples, channels, x_length, _ = activation.shape
    channels_in, modes_y, modes_x = spectral_weight.shape[:3]
    width = samples // groups * modes_x
    return (
        slabs == 4
        and groups & (groups - 1) == 0
        and modes_y // slabs == 8
        and modes_x == 2 * BLOCK
        and width == 128
        and x_length // slabs % 16 == 0
        and channels % 16 == 0
        and channels_in % groups == 0
        and channels_in % 8 == 0
    )


def solution(mesh):
    placed = (P("dp", None, "slab", None), P("dp", None, "slab", None), P(None, "slab", None, None))
    results = (P("dp", None, "slab", None), P("dp", "slab", None, None))

    def spread_over(body):
        return jax.shard_map(
            body, mesh=mesh, in_specs=placed, out_specs=results, check_vma=False
        )

    def scheduled(*values):
        return fast_body(*values)


    def run(activation, cotangent, spectral_weight):
        return spread_over(scheduled if fits(mesh, activation, spectral_weight) else plain_body)(
            activation, cotangent, spectral_weight
        )

    return run
```
